256 devices in a mesh: seq: 8 (over y, z_lo), exp: 32 (over x, z_hi, core).
Axes of the slice: x: 4, y: 4, z: 8 (z_hi: 4, z_lo: 2; z = z_hi * 2 + z_lo), core: 2. Of those that a mesh axis runs over, the one named last changes fastest.
Arguments:
- tokens: bfloat16 [16384, 4096], P(('seq', 'exp')), may hold values from -6 to 6
- norm_gain: float32 [4096], replicated, may hold values from 0.1 to 1.9
- queries: bfloat16 [16384, 2048], P(('seq', 'exp')), may hold values from -24 to 24
- attn_keys: bfloat16 [16384, 2048], P(('seq', 'exp')), may hold values from -4.5 to 4.5
- attn_values: bfloat16 [16384, 2048], P(('seq', 'exp')), may hold values from -6 to 6
- expert_ids: int32 [16384, 2], P(('seq', 'exp')), may hold values from 0 to 63, all different within a row; in each aligned block of 64 rows (0 to 63, 64 to 127, ...) at most 2 rows name the same one
- route_weights: float32 [16384, 2], P(('seq', 'exp')), may hold values from 0.1 to 1
- gate_proj: bfloat16 [64, 1408, 4096], P('exp', 'seq'), may hold values from -0.09375 to 0.09375
- up_proj: bfloat16 [64, 1408, 4096], P('exp', 'seq'), may hold values from -0.09375 to 0.09375
- down_proj: bfloat16 [64, 1408, 4096], P('exp', 'seq'), may hold values from -0.15625 to 0.15625
Outputs:
- attention: bfloat16 [16384, 2048], P(('seq', 'exp'))
- expert_mix: bfloat16 [16384, 4096], P(('seq', 'exp'))
The draws below stay inside these ranges and needn't reach their ends.
Inputs may be any that keep to these rules, and one draw needn't show every extreme that they name: `expert_ids`: the two experts of a token differ. Among the rows of one device (64 consecutive tokens, aligned), every expert is named exactly 2 times.
All inputs are finite; a program needn't handle non-finite values.
Results may differ from the reference program's by a relative error of at most 0.015.
Values may be sent and summed in bfloat16 or wider, within the bound.
A program may use at most 128 MiB of HBM per device.

```python
import math
import jax
import jax.numpy as jnp
import numpy as np
from jax import lax

D = 4096
FF = 1408
EXPERTS = 64
HEADS = 32
HDIM = 64
SUMS = 64
CAP = 2
TOK_DEV = 64
TOKENS = 16384
SEG_LEN = 1024
SEGS = 16
BLK = 16
ATT = 2048
FF_DEV = 176
N_SEQ = 8


def key_parts(key):
    base_key = jax.random.fold_in(key, 71)
    key_one = jax.random.fold_in(base_key, 0)
    drawn_vals = jnp.clip(jax.random.normal(key_one, (TOKENS, ATT), jnp.float32), -4.5, 4.5)
    return drawn_vals


def draw_attn_keys(key, part):
    drawn_vals = key_parts(key)
    return drawn_vals.astype(jnp.bfloat16)


def draw_queries(key, part):
    query_key = jax.random.fold_in(key, 29)
    query_vals = jnp.clip(jax.random.normal(query_key, (TOKENS, ATT), jnp.float32), -6.0, 6.0)
    return query_vals.astype(jnp.bfloat16)


def block_levels(key, extent, shards, least, largest):
    gain, own = 1.0, jax.random.fold_in(key, 6)
    for dim, blocks in shards:
        draws = jnp.exp(jax.random.uniform(jax.random.fold_in(own, dim), (blocks,), jnp.float32, least / len(shards), largest / len(shards)))
        gain = gain * jnp.repeat(draws, extent[dim] // blocks).reshape([-1 if axis == dim else 1 for axis in range(len(extent))])
    return gain


def routed_block(own_key, own, number, rows, count, top, bound, skew):
    order = jax.random.permutation(own_key, count)
    packed, common = portions_of(count, rows * top, bound, skew, True), portions_of(count, rows * top, bound, skew, False)
    places = jnp.arange(count)

    def named(sizes, rotation):
        used = int((sizes > 0).sum())
        fixed = max(1, used // 4)
        moved = fixed + (places - fixed + rotation * (used - fixed)) % max(1, count - fixed)
        return jnp.zeros((count,), jnp.int32).at[order[jnp.where(places < fixed, places, moved)]].set(jnp.asarray(sizes, jnp.int32))

    sizes = jnp.where(number % 4 == 0, named(packed, number // 4), named(common, number - number // 4 - 1))
    mixed = jax.random.permutation(jax.random.fold_in(own, 3), count)
    source_of, taker = mixed[0:count // 2 * 2:2], mixed[1:count // 2 * 2:2]
    room = jnp.minimum(sizes[source_of] - 1, bound - sizes[taker]) // 2
    room = jnp.where((source_of == order[0]) | (taker == order[0]) | (sizes[taker] == 0), 0, jnp.maximum(room, 0))
    moved = jax.random.randint(jax.random.fold_in(own, 4), (count // 2,), 0, 1 << 20) % (room + 1)
    sizes = sizes.at[source_of].add(-moved).at[taker].add(moved)
    items = jnp.searchsorted(jnp.cumsum(sizes), jnp.arange(rows * top), side="right").astype(jnp.int32)
    table = items.reshape(top, rows).T
    table = table[jax.random.permutation(jax.random.fold_in(own, 1), rows)]
    rotation = jax.random.randint(jax.random.fold_in(own, 2), (rows, 1), 0, top)
    return jnp.take_along_axis(table, (jnp.arange(top)[None, :] + rotation) % top, axis=1)


def portions_of(count, total, bound, lean, full):
    loads = [(1 << 20) // math.isqrt(rank ** lean) + 1 for rank in range(1, count + 1)]
    largest = bound if full else min(bound, max(-(-total // count), total * loads[0] // sum(loads)))
    least = 1 if total - largest >= count - 1 else 0
    given, spare = [largest] + [least] * (count - 1), total - largest - least * (count - 1)
    while spare > 0:
        free = [i for i in range(1, count) if given[i] < largest] or [i for i in range(1, count) if given[i] < bound]
        pool, remaining = sum([loads[i] for i in free]), spare
        for i in free:
            more = min(bound - given[i], max(1, remaining * loads[i] // pool), spare)
            given[i] = given[i] + more
            spare = spare - more
    return np.array(given)


def scatter_about(stream_key, dims, width, most, shards=(), kind=jnp.bfloat16):
    values = jax.random.normal(stream_key, dims, jnp.float32) * width
    if len(shards) > 0:
        values = block_levels(stream_key, dims, shards, -0.22, 0.18) * values
    return jnp.clip(values, min=-most, max=most).astype(kind)


def setup_inputs(seed: int = 0) -> dict:
    keys = jax.random.split(jax.random.key(seed), 11)
    tokens = scatter_about(keys[0], (TOKENS, D), 1.0, 6.0, ((0, 256),))
    norm_gain = jnp.clip(1.0 + 0.18 * jax.random.normal(keys[1], (D,), jnp.float32), 0.1, 1.9)
    queries = draw_queries(jax.random.fold_in(keys[10], 71), 0)
    attn_keys = draw_attn_keys(jax.random.fold_in(keys[10], 71), 0)
    attn_values = scatter_about(keys[4], (TOKENS, ATT), 1.0, 6.0, ((0, 256),))
    expert_ids_keys = jax.random.split(jax.random.fold_in(keys[5], 1), TOKENS // TOK_DEV)
    expert_ids_turns = jax.random.permutation(jax.random.fold_in(keys[5], 3), TOKENS // TOK_DEV)
    expert_ids = jax.vmap(lambda own, number: routed_block(jax.random.fold_in(keys[5], 2), own, number, TOK_DEV, EXPERTS, 2, CAP, 2))(expert_ids_keys, expert_ids_turns).reshape((TOKENS, 2))
    route_weights = jnp.clip(0.1 + 0.9 * jax.random.uniform(keys[6], (TOKENS, 2), jnp.float32) ** block_levels(keys[6], (TOKENS, 2), ((0, 256),), -0.2, 0.2), 0.1, 1.0)
    gate_proj = scatter_about(keys[7], (EXPERTS, FF, D), D ** -0.5, 0.09375, ((0, 32), (1, 8)))
    up_proj = scatter_about(keys[8], (EXPERTS, FF, D), D ** -0.5, 0.09375, ((0, 32), (1, 8)))
    down_proj = scatter_about(keys[9], (EXPERTS, FF, D), FF ** -0.5, 0.15625, ((0, 32), (1, 8)))
    return dict(tokens=tokens, norm_gain=norm_gain, queries=queries, attn_keys=attn_keys, attn_values=attn_values, expert_ids=expert_ids, route_weights=route_weights, gate_proj=gate_proj, up_proj=up_proj, down_proj=down_proj)


EPS = 1e-05
NEG = -1e+30
HIGH = lax.Precision.HIGHEST

def normalize(tokens, norm_gain):
    values = tokens.astype(jnp.float32)
    inv_rms = lax.rsqrt(lax.optimization_barrier(jnp.mean(values * values, axis=-1, keepdims=True)) + EPS)
    return (values * inv_rms * norm_gain.astype(jnp.float32)).astype(jnp.bfloat16)

def summarize(block_vals):
    values = block_vals.astype(jnp.float32).reshape(SEGS, SUMS, BLK, HDIM)
    summed = lax.optimization_barrier(jnp.sum(values, axis=2)) * (1.0 / math.sqrt(BLK))
    return summed.astype(jnp.bfloat16).reshape(SEGS * SUMS, 1, HDIM)

def attend(query_blk, seg_keys, seg_values, sum_keys, sum_values, segment):
    score_scale = 1.0 / math.sqrt(HDIM)
    query_f = query_blk.astype(jnp.float32)
    local_sc = jnp.einsum('qhd,khd->hqk', query_f, seg_keys.astype(jnp.float32), precision=HIGH) * score_scale
    summ_sc = jnp.einsum('qhd,khd->hqk', query_f, sum_keys.astype(jnp.float32), precision=HIGH) * score_scale
    query_pos = jnp.arange(query_blk.shape[0], dtype=jnp.int32)
    key_pos = jnp.arange(seg_keys.shape[0], dtype=jnp.int32)
    local_ok = key_pos[None, :] <= query_pos[:, None]
    summ_ok = jnp.arange(sum_keys.shape[0], dtype=jnp.int32) // SUMS < segment
    local_sc = jnp.where(local_ok[None], local_sc, NEG)
    summ_sc = jnp.where(summ_ok[None, None], summ_sc, NEG)
    top_sc = jnp.maximum(lax.optimization_barrier(jnp.max(local_sc, axis=-1, keepdims=True)), lax.optimization_barrier(jnp.max(summ_sc, axis=-1, keepdims=True)))
    local_ex = jnp.exp(local_sc - top_sc)
    summ_ex = jnp.exp(summ_sc - top_sc)
    totals = lax.optimization_barrier(jnp.sum(local_ex, axis=-1, keepdims=True)) + lax.optimization_barrier(jnp.sum(summ_ex, axis=-1, keepdims=True))
    local_wt = (local_ex / totals).astype(jnp.bfloat16).astype(jnp.float32)
    summ_wt = (summ_ex / totals).astype(jnp.bfloat16).astype(jnp.float32)
    mixed_out = jnp.einsum('hqk,khd->qhd', local_wt, seg_values.astype(jnp.float32), precision=HIGH)
    return mixed_out + jnp.einsum('hqk,khd->qhd', summ_wt, sum_values.astype(jnp.float32), precision=HIGH)

def reference(tokens, norm_gain, queries, attn_keys, attn_values, expert_ids, route_weights, gate_proj, up_proj, down_proj):
    normed = normalize(tokens, norm_gain)

    def heads_major(array):
        return array.reshape(SEGS, SEG_LEN, HEADS, HDIM).transpose(2, 0, 1, 3)

    def per_head(inputs):
        head_q, head_k, head_v = inputs
        sum_keys = summarize(head_k)
        sum_values = summarize(head_v)

        def per_seg(seg_index):
            return attend(head_q[seg_index][:, None, :], head_k[seg_index][:, None, :], head_v[seg_index][:, None, :], sum_keys, sum_values, seg_index)
        return lax.map(per_seg, jnp.arange(SEGS, dtype=jnp.int32))
    head_out = lax.map(per_head, (heads_major(queries), heads_major(attn_keys), heads_major(attn_values)))
    head_out = head_out.astype(jnp.bfloat16)[:, :, :, 0, :]
    attention = head_out.transpose(1, 2, 0, 3).reshape(TOKENS, HEADS * HDIM)
    block_count = TOKENS // TOK_DEV
    id_blocks = expert_ids.reshape(block_count, TOK_DEV * 2)
    onehot = (id_blocks[:, :, None] == jnp.arange(EXPERTS, dtype=jnp.int32)[None, None, :]).astype(jnp.int32)
    before = jnp.cumsum(onehot, axis=1) - onehot
    slot_ids = lax.optimization_barrier(jnp.sum(before * onehot, axis=2))
    row_pos = jnp.arange(block_count, dtype=jnp.int32)[:, None] * CAP + slot_ids
    token_of = (jnp.arange(TOKENS * 2, dtype=jnp.int32) // 2).reshape(block_count, TOK_DEV * 2)
    row_table = jnp.full((EXPERTS, block_count * CAP), TOKENS, jnp.int32)
    row_table = row_table.at[id_blocks.reshape(-1), row_pos.reshape(-1)].set(token_of.reshape(-1))
    weight_table = jnp.zeros((EXPERTS, block_count * CAP), jnp.float32)
    weight_table = weight_table.at[id_blocks.reshape(-1), row_pos.reshape(-1)].set(route_weights.reshape(-1).astype(jnp.float32))
    padded = jnp.concatenate([normed, jnp.zeros((1, D), jnp.bfloat16)], axis=0)

    def per_expert(running, inputs):
        table_e, weight_e, gate_e, up_e, down_e = inputs
        rows_e = padded[table_e]
        gate_act = jnp.dot(rows_e, gate_e.T, preferred_element_type=jnp.float32)
        up_act = jnp.dot(rows_e, up_e.T, preferred_element_type=jnp.float32)
        hidden = (jax.nn.silu(gate_act) * up_act).astype(jnp.bfloat16)
        piece_list = []
        for block_index in range(N_SEQ):
            lower = block_index * FF_DEV
            piece = jnp.dot(hidden[:, lower:lower + FF_DEV], down_e[lower:lower + FF_DEV], preferred_element_type=jnp.float32)
            piece_list.append(lax.optimization_barrier(piece.astype(jnp.bfloat16)).astype(jnp.float32))
        total_sum = piece_list[0]
        for piece in piece_list[1:]:
            total_sum = total_sum + piece
        expert_out = lax.optimization_barrier(total_sum.astype(jnp.bfloat16)).astype(jnp.float32)
        running = running.at[table_e].add(weight_e[:, None] * expert_out, mode='drop')
        return (running, None)
    running, unused = lax.scan(per_expert, jnp.zeros((TOKENS, D), jnp.float32), (row_table, weight_table, gate_proj, up_proj, down_proj))
    return (attention, running.astype(jnp.bfloat16))
```

```python
import functools

import jax
import jax.numpy as jnp
from jax import lax
from jax.experimental import pallas as pl
from jax.experimental.pallas import tpu as pltpu
from jax.sharding import PartitionSpec as P

MESH = pl.DeviceIdType.MESH
BF = jnp.bfloat16
F32 = jnp.float32
EPS = 1e-05
NEG = -1e30

D = 4096
W = 1024
FFD = 176
FFP = 256
NT = (((1,), (1,)), ((), ()))

GATHER = (
    (0, 0, 64, 64, "p"),
    (0, 0, 256, 64, "+"),
    (0, 64, 320, 64, "+"),
    (0, 0, 128, 64, "-"),
    (0, 64, 192, 64, "-"),
    (0, 256, 384, 64, "+"),
    (0, 192, 448, 64, "-"),
    (1, 0, 256, 64, "+"),
    (1, 0, 128, 64, "-"),
    (1, 256, 384, 32, "+"),
    (1, 160, 416, 32, "-"),
    (1, 0, 64, 64, "p"),
    (1, 256, 320, 64, "p"),
    (1, 128, 192, 64, "p"),
    (1, 384, 448, 32, "p"),
    (1, 416, 480, 32, "p"),
)
REDUCE = (
    (0, 384, 64, "+"),
    (0, 448, 64, "-"),
    (0, 192, 64, "+"),
    (0, 128, 64, "+"),
    (0, 256, 64, "-"),
    (0, 320, 64, "-"),
    (0, 64, 64, "p"),
    (1, 448, 64, "p"),
    (1, 192, 64, "p"),
    (1, 320, 64, "p"),
    (1, 64, 64, "p"),
    (1, 384, 32, "+"),
    (1, 416, 32, "-"),
    (1, 128, 64, "+"),
    (1, 256, 64, "-"),
)


def iota(shape, dim):
    return lax.broadcasted_iota(jnp.int32, shape, dim)


def dot(a, b):
    return jnp.dot(a, b, preferred_element_type=F32)


def remote(src, dst, send, recv, device):
    return pltpu.make_async_remote_copy(
        src_ref=src,
        dst_ref=dst,
        send_sem=send,
        recv_sem=recv,
        device_id=device,
        device_id_type=MESH,
    )


def kernel(
    tok, gain, q, k, v, ids_t, ids, rw, gp, up, dp,
    att_out, mix_out,
    n4, sb, ab, xg, pb, wg, wu, wd, rb, f4, fb, cb,
    qb, kb, vb, smk, smv, ob, ao,
    w_sem, d_send, d_recv, c_send, c_recv, g_send, g_recv, r_send, r_recv,
    a_send, a_recv, s_send, s_recv, o_send, o_recv,
):
    me_s = lax.axis_index("seq")
    me_p = lax.axis_index("exp")
    me_y = lax.div(me_s, 2)
    me_z = lax.rem(me_s, 2)
    core = lax.rem(me_p, 2)
    chip = lax.div(me_p, 2)
    half = lax.div(me_p, 16)
    slot = lax.rem(me_p, 16)
    seg = 2 * me_s + core
    peer = {
        "+": (2 * lax.rem(me_y + 1, 4) + me_z, me_p),
        "-": (2 * lax.rem(me_y + 3, 4) + me_z, me_p),
        "p": (2 * me_y + 1 - me_z, me_p),
    }

    weights = [
        pltpu.make_async_copy(src, dst.at[:, pl.ds(0, FFD), :], w_sem.at[i])
        for i, (src, dst) in enumerate(((gp, wg), (up, wu), (dp, wd)))
    ]
    for copy in weights:
        copy.start()

    barrier = pltpu.get_barrier_semaphore()

    def greet_exp(j, carry):
        pl.semaphore_signal(
            barrier, inc=1, device_id=(me_s, lax.rem(me_p + j, 32)), device_id_type=MESH
        )
        return carry

    def greet_seq(j, carry):
        other = lax.rem(me_s + j, 8)
        pl.semaphore_signal(barrier, inc=1, device_id=(other, me_p), device_id_type=MESH)
        pl.semaphore_signal(
            barrier, inc=1, device_id=(other, me_p + 1 - 2 * core), device_id_type=MESH
        )
        return carry

    lax.fori_loop(1, 32, greet_exp, 0)
    lax.fori_loop(1, 8, greet_seq, 0)

    def norm_rows(i, carry):
        rows = pl.ds(pl.multiple_of(i * 16, 16), 16)
        vals = tok[rows, :].astype(F32)
        inv = lax.rsqrt(jnp.mean(vals * vals, axis=-1, keepdims=True) + EPS)
        normed = (vals * inv * gain[...]).astype(BF)
        for c in range(4):
            n4[pl.ds(pl.multiple_of(c * 64 + i * 16, 16), 16), :] = normed[:, c * W : c * W + W]
        return carry

    lax.fori_loop(0, 4, norm_rows, 0)

    row_j = iota((512, 64), 0)
    expert_j = 2 * (row_j // 16) + (row_j // 2) % 2
    named = ((ids_t[0:1, :] == expert_j) | (ids_t[1:2, :] == expert_j)).astype(F32)
    above = (iota((64, 64), 0) < iota((64, 64), 1)).astype(BF)
    before = dot(named.astype(BF), above)
    pick = jnp.where(before == (row_j % 2).astype(F32), named, 0.0)
    block_j = (row_j // 4) % 4
    pick4 = jnp.concatenate([jnp.where(block_j == c, pick, 0.0).astype(BF) for c in range(4)], axis=1)
    for n in range(2):
        cols = pl.ds(n * 512, 512)
        sb[:, cols] = dot(pick4, n4[:, cols]).astype(BF)

    pl.semaphore_wait(barrier, 45)

    def block_of(index):
        return pl.ds(pl.multiple_of(index * 16, 16), 16)

    def exchange(src, dst, send, recv):
        def start(j, carry):
            to = lax.rem(me_p + j, 32)
            remote(
                src.at[block_of(to), :], dst.at[block_of(me_p), :],
                send.at[to], recv.at[me_p], (me_s, to),
            ).start()
            return carry

        lax.fori_loop(1, 32, start, 0)

    def exchange_wait(src, dst, send, recv, sent):
        def wait(j, carry):
            other = lax.rem(me_p + j, 32)
            copy = remote(
                src.at[block_of(other), :], dst.at[block_of(other), :],
                send.at[other], recv.at[other], (me_s, other),
            )
            if sent:
                copy.wait_send()
            else:
                copy.wait_recv()
            return carry

        lax.fori_loop(1, 32, wait, 0)

    exchange(sb, ab, d_send, d_recv)

    def cols_of(index):
        return pl.ds(pl.multiple_of(index * 128, 128), 128)

    def toks_of(index):
        return pl.ds(pl.multiple_of(index * 64, 64), 64)

    def heads_start(j, carry):
        m = lax.rem(chip + j, 16)
        to = 2 * m + half
        for i, (src, dst) in enumerate(((k, kb), (v, vb), (q, qb))):
            piece, land = src.at[:, cols_of(m)], dst.at[toks_of(slot), :]

            @pl.when(to != me_p)
            def _():
                remote(piece, land, a_send.at[i, m], a_recv.at[i, slot], (me_s, to)).start()

            @pl.when(to == me_p)
            def _():
                pltpu.make_async_copy(piece, land, a_recv.at[i, slot]).start()

        return carry

    lax.fori_loop(0, 16, heads_start, 0)

    def heads_wait(j, carry):
        for i, dst in enumerate((kb, vb, qb)):
            land = dst.at[toks_of(j), :]
            pltpu.make_async_copy(land, land, a_recv.at[i, j]).wait()
        return carry

    def heads_sent(j, carry):
        for i, (src, dst) in enumerate(((k, kb), (v, vb), (q, qb))):

            @pl.when(2 * j + half != me_p)
            def _():
                remote(
                    src.at[:, cols_of(j)], dst.at[toks_of(slot), :],
                    a_send.at[i, j], a_recv.at[i, slot], (me_s, 2 * j + half),
                ).wait_send()

        return carry

    def zero_rows(i, carry):
        rows = pl.ds(pl.multiple_of(FFD + i * 16, 16), 16)
        for e in range(2):
            for ref in (wg, wu, wd):
                ref[e, rows, :] = jnp.zeros((16, D), BF)
        return carry

    lax.fori_loop(0, 5, zero_rows, 0)

    ab[block_of(me_p), :] = sb[block_of(me_p), :]
    exchange_wait(sb, ab, d_send, d_recv, False)
    out_i, in_i = iota((128, 512), 0), iota((128, 512), 1)
    home = ((out_i % 64) // 2) * 16 + (out_i // 64) * 2 + out_i % 2

    for c in range(4):
        order = (in_i == home + 4 * c).astype(BF)
        rows = dot(order, ab[...]).astype(BF)
        xg[0, 0:64, c * W : c * W + W] = rows[0:64]
        xg[1, 0:64, c * W : c * W + W] = rows[64:128]

    def gather(i):
        e, src, dst, n, way = GATHER[i]
        return remote(
            xg.at[e, pl.ds(src, n), :], xg.at[e, pl.ds(dst, n), :],
            g_send.at[i], g_recv.at[i], peer[way],
        )

    def arrived(i):
        e, _, dst, n, way = GATHER[i]
        ref = xg.at[e, pl.ds(dst, n), :]
        remote(ref, ref, g_send.at[i], g_recv.at[i], peer[way]).wait_recv()

    for i in (0, 7, 8, 1, 3, 11):
        gather(i).start()

    lax.fori_loop(0, 16, heads_wait, 0)
    blocks = (iota((64, 1024), 1) // 16 == iota((64, 1024), 0)).astype(BF)
    mine = toks_of(seg)
    smk[mine, :] = (dot(blocks, kb[...]) * 0.25).astype(BF)
    smv[mine, :] = (dot(blocks, vb[...]) * 0.25).astype(BF)

    def sums(g, src_seg):
        other = (lax.div(g, 2), 2 * chip + lax.rem(g, 2))
        for i, ref in enumerate((smk, smv)):
            yield remote(
                ref.at[toks_of(src_seg), :], ref.at[toks_of(src_seg), :],
                s_send.at[i, g], s_recv.at[i, src_seg], other,
            )

    def sums_start(g, carry):
        for copy in sums(g, seg):
            copy.start()
        return carry

    def sums_sent(g, carry):
        for copy in sums(g, seg):
            copy.wait_send()
        return carry

    def sums_wait(g, carry):
        for copy in sums(g, g):
            copy.wait_recv()
        return carry

    def sums_zero(g, carry):
        smk[toks_of(g), :] = jnp.zeros((64, 128), BF)
        smv[toks_of(g), :] = jnp.zeros((64, 128), BF)
        return carry

    lax.fori_loop(seg + 1, 16, sums_start, 0)
    lax.fori_loop(seg + 1, 16, sums_zero, 0)

    arrived(0)
    gather(2).start()
    gather(4).start()
    arrived(7)
    gather(9).start()
    gather(12).start()
    arrived(8)
    gather(10).start()
    gather(13).start()

    lax.fori_loop(0, seg, sums_wait, 0)

    def attend(step, carry):
        rows = pl.ds(pl.multiple_of(lax.div(step, 2) * 128, 128), 128)
        head = lax.rem(step, 2)
        lane = iota((128, 128), 1) // 64 == head
        query = jnp.where(lane, qb[rows, :].astype(F32) * 0.125, 0.0).astype(BF)
        local = lax.dot_general(query, kb[...], NT, preferred_element_type=F32)
        summ = lax.dot_general(query, smk[...], NT, preferred_element_type=F32)
        pos = lax.div(step, 2) * 128 + iota((128, 1024), 0)
        col = iota((128, 1024), 1)
        local = jnp.where(col <= pos, local, NEG)
        summ = jnp.where(col < seg * 64, summ, NEG)
        top = jnp.maximum(
            jnp.max(local, axis=-1, keepdims=True), jnp.max(summ, axis=-1, keepdims=True)
        )
        local = jnp.exp(local - top)
        summ = jnp.exp(summ - top)
        total = jnp.sum(local, axis=-1, keepdims=True) + jnp.sum(summ, axis=-1, keepdims=True)
        mixed = (dot(local.astype(BF), vb[...]) + dot(summ.astype(BF), smv[...])) / total
        ob[rows, :] = jnp.where(lane, mixed, ob[rows, :].astype(F32)).astype(BF)
        return carry

    ob[...] = jnp.zeros((1024, 128), BF)
    lax.fori_loop(0, 8, attend, 0)
    arrived(1)
    gather(5).start()
    arrived(4)
    gather(6).start()
    arrived(9)
    gather(14).start()
    arrived(10)
    gather(15).start()
    lax.fori_loop(8, 16, attend, 0)

    def back_start(j, carry):
        i = lax.rem(slot + j, 16)
        to = 16 * core + i
        piece, land = ob.at[toks_of(i), :], ao.at[:, cols_of(chip)]

        @pl.when(to != me_p)
        def _():
            remote(piece, land, o_send.at[i], o_recv.at[chip], (me_s, to)).start()

        @pl.when(to == me_p)
        def _():
            pltpu.make_async_copy(piece, land, o_recv.at[chip]).start()

        return carry

    def back_wait(m, carry):
        land = ao.at[:, cols_of(m)]
        pltpu.make_async_copy(land, land, o_recv.at[m]).wait()
        return carry

    def back_sent(i, carry):
        @pl.when(16 * core + i != me_p)
        def _():
            remote(
                ob.at[toks_of(i), :], ao.at[:, cols_of(chip)],
                o_send.at[i], o_recv.at[chip], (me_s, 16 * core + i),
            ).wait_send()

        return carry

    lax.fori_loop(0, 16, back_start, 0)

    def expert(e, group):
        rows = pl.ds(pl.multiple_of(group * 128, 128), 128)
        gate = jnp.zeros((128, FFP), F32)
        high = jnp.zeros((128, FFP), F32)
        for c in range(4):
            part = xg[e, rows, c * W : c * W + W]
            gate += lax.dot_general(
                part, wg[e, :, c * W : c * W + W], NT, preferred_element_type=F32
            )
            high += lax.dot_general(
                part, wu[e, :, c * W : c * W + W], NT, preferred_element_type=F32
            )
        hidden = (gate / (1.0 + jnp.exp(-gate)) * high).astype(BF)
        for c in range(8):
            pb[e, rows, c * 512 : c * 512 + 512] = dot(
                hidden, wd[e, :, c * 512 : c * 512 + 512]
            ).astype(BF)

    def experts(first, groups):
        def step(i, carry):
            expert(lax.rem(i, 2), first + lax.div(i, 2))
            return carry

        lax.fori_loop(0, 2 * groups, step, 0)

    def reduce(i):
        e, src, n, way = REDUCE[i]
        return remote(
            pb.at[e, pl.ds(src, n), :], rb.at[i, pl.ds(0, n), :],
            r_send.at[i], r_recv.at[i], peer[way],
        )

    def landed(i):
        _, _, n, way = REDUCE[i]
        ref = rb.at[i, pl.ds(0, n), :]
        remote(ref, ref, r_send.at[i], r_recv.at[i], peer[way]).wait_recv()

    def add_into(e, first, n, *terms):
        def step(i, carry):
            rows = pl.ds(pl.multiple_of(first + i * 16, 16), 16)
            total = pb[e, rows, :].astype(F32)
            for term in terms:
                total += rb[term, pl.ds(pl.multiple_of(i * 16, 16), 16), :].astype(F32)
            pb[e, rows, :] = total.astype(BF)
            return carry

        lax.fori_loop(0, n // 16, step, 0)

    def finish(e, *terms):
        def step(i, carry):
            rows = pl.ds(pl.multiple_of(i * 16, 16), 16)
            total = pb[e, rows, :].astype(F32)
            for term in terms:
                total += rb[term, rows, :].astype(F32)
            total = total.astype(BF)
            for c in range(4):
                place = pl.ds(pl.multiple_of(c * 128 + e * 64 + i * 16, 16), 16)
                f4[place, :] = total[:, c * W : c * W + W]
            return carry

        lax.fori_loop(0, 4, step, 0)

    for copy in weights:
        copy.wait()
    arrived(11)
    experts(0, 1)
    reduce(10).start()
    arrived(2)
    arrived(3)
    arrived(12)
    arrived(13)
    experts(1, 2)
    for i in (2, 4, 8, 9):
        reduce(i).start()
    arrived(5)
    arrived(6)
    arrived(14)
    arrived(15)
    experts(3, 1)
    for i in (0, 1, 7):
        reduce(i).start()

    landed(8)
    add_into(1, 128, 64, 8)
    landed(9)
    add_into(1, 256, 64, 9)
    landed(7)
    add_into(1, 384, 64, 7)
    reduce(11).start()
    reduce(12).start()
    landed(0)
    add_into(0, 128, 64, 0)
    reduce(3).start()
    landed(1)
    add_into(0, 320, 64, 1)
    reduce(5).start()
    landed(11)
    add_into(1, 128, 32, 11)
    reduce(13).start()
    landed(12)

    def add_upper(i, carry):
        rows = pl.ds(pl.multiple_of(288 + i * 16, 16), 16)
        part = rb[12, pl.ds(pl.multiple_of(i * 16, 16), 16), :].astype(F32)
        pb[1, rows, :] = (pb[1, rows, :].astype(F32) + part).astype(BF)
        return carry

    lax.fori_loop(0, 2, add_upper, 0)
    reduce(14).start()
    landed(2)
    landed(5)
    add_into(0, 64, 64, 2, 5)
    reduce(6).start()
    landed(10)
    landed(13)
    landed(14)
    finish(1, 10, 13, 14)
    landed(3)
    landed(4)
    landed(6)
    finish(0, 3, 4, 6)

    out_o, in_o = iota((512, 512), 0), iota((512, 512), 1)
    place = ((out_o // 4) % 4) * 128 + ((out_o // 2) % 2) * 64 + (out_o // 16) * 2 + out_o % 2
    order = (in_o == place).astype(BF)
    for n in range(2):
        cols = pl.ds(n * 512, 512)
        fb[:, cols] = dot(order, f4[:, cols]).astype(BF)
    exchange(fb, cb, c_send, c_recv)
    cb[block_of(me_p), :] = fb[block_of(me_p), :]

    col_j = iota((64, 512), 1)
    expert_c = 2 * (col_j // 16) + (col_j // 2) % 2
    first = ids[:, 0:1] == expert_c
    second = ids[:, 1:2] == expert_c
    named_c = (first | second).astype(BF)
    below = (iota((64, 64), 1) < iota((64, 64), 0)).astype(BF)
    before_c = dot(below, named_c)
    share = jnp.where(first, rw[:, 0:1], 0.0) + jnp.where(second, rw[:, 1:2], 0.0)
    share = jnp.where(before_c == (col_j % 2).astype(F32), share, 0.0)
    big = share.astype(BF)
    small = (share - big.astype(F32)).astype(BF)
    block_c = (col_j // 4) % 4

    lax.fori_loop(0, 16, back_wait, 0)
    att_out[...] = ao[...]

    exchange_wait(fb, cb, c_send, c_recv, False)
    none = jnp.zeros((64, 512), BF)
    for c in range(4):
        mix = dot(jnp.where(block_c == c, big, none), cb[...])
        mix += dot(jnp.where(block_c == c, small, none), cb[...])
        mix_out[:, c * W : c * W + W] = mix.astype(BF)

    exchange_wait(sb, ab, d_send, d_recv, True)
    exchange_wait(fb, cb, c_send, c_recv, True)
    lax.fori_loop(0, 16, heads_sent, 0)
    lax.fori_loop(0, 16, back_sent, 0)
    lax.fori_loop(seg + 1, 16, sums_sent, 0)
    for i in range(len(GATHER)):
        gather(i).wait_send()
    for i in range(len(REDUCE)):
        reduce(i).wait_send()


def on_device(tokens, gain, queries, keys, values, ids, rw, gate, up, down):
    vmem = pl.BlockSpec(memory_space=pltpu.VMEM)
    hbm = pl.BlockSpec(memory_space=pl.ANY)
    dma = pltpu.SemaphoreType.DMA
    return pl.pallas_call(
        kernel,
        out_shape=(
            jax.ShapeDtypeStruct((64, 2048), BF),
            jax.ShapeDtypeStruct((64, D), BF),
        ),
        in_specs=[vmem, vmem, hbm, hbm, hbm, vmem, vmem, vmem, hbm, hbm, hbm],
        out_specs=(vmem, vmem),
        scratch_shapes=[
            pltpu.VMEM((256, W), BF),
            pltpu.VMEM((512, W), BF),
            pltpu.VMEM((512, W), BF),
            pltpu.VMEM((2, 512, D), BF),
            pltpu.VMEM((2, 512, D), BF),
            pltpu.VMEM((2, FFP, D), BF),
            pltpu.VMEM((2, FFP, D), BF),
            pltpu.VMEM((2, FFP, D), BF),
            pltpu.VMEM((15, 64, D), BF),
            pltpu.VMEM((512, W), BF),
            pltpu.VMEM((512, W), BF),
            pltpu.VMEM((512, W), BF),
            pltpu.VMEM((1024, 128), BF),
            pltpu.VMEM((1024, 128), BF),
            pltpu.VMEM((1024, 128), BF),
            pltpu.VMEM((1024, 128), BF),
            pltpu.VMEM((1024, 128), BF),
            pltpu.VMEM((1024, 128), BF),
            pltpu.VMEM((64, 2048), BF),
            dma((3,)),
            dma((32,)),
            dma((32,)),
            dma((32,)),
            dma((32,)),
            dma((len(GATHER),)),
            dma((len(GATHER),)),
            dma((len(REDUCE),)),
            dma((len(REDUCE),)),
            dma((3, 16)),
            dma((3, 16)),
            dma((2, 16)),
            dma((2, 16)),
            dma((16,)),
            dma((16,)),
        ],
        compiler_params=pltpu.CompilerParams(
            collective_id=0, has_side_effects=True, vmem_limit_bytes=60 * 1024 * 1024
        ),
        name="layer",
    )(tokens, gain.reshape(1, D), queries, keys, values, ids.T, ids, rw, gate, up, down)


def solution(mesh):
    rows = P(("seq", "exp"), None)
    parts = P("exp", "seq", None)
    return jax.shard_map(
        on_device,
        mesh=mesh,
        in_specs=(rows, P(), rows, rows, rows, rows, rows, parts, parts, parts),
        out_specs=(rows, rows),
        check_vma=False,
    )
```

```python
import functools

import jax
import jax.numpy as jnp
from jax import lax
from jax.experimental import pallas as pl
from jax.experimental.pallas import tpu as pltpu
from jax.sharding import PartitionSpec as P

MESH = pl.DeviceIdType.MESH
BF = jnp.bfloat16
F32 = jnp.float32
EPS = 1e-05
NEG = -1e30

D = 4096
W = 256
FFD = 176
FFP = 256
NT = (((1,), (1,)), ((), ()))

STREAMS = ((0, 0, 32, True), (0, 32, 32, True), (1, 0, 32, True), (1, 32, 32, False))


def plan():
    gather, reduce = {}, {}
    for t, (e, off, n, z_first) in enumerate(STREAMS):
        h = n // 2

        def at(group, z, off=off):
            return group * 128 + z * 64 + off

        g = {
            "p": (at(0, 0), at(0, 1), n, "p"),
            "+o": (at(0, 0), at(2, 0), n, "+"),
            "-o": (at(0, 0), at(1, 0), n, "-"),
        }
        if z_first:
            g["+x"] = (at(0, 1), at(2, 1), n, "+")
            g["-x"] = (at(0, 1), at(1, 1), n, "-")
            g["+f"] = (at(2, 0), at(3, 0), n, "+")
            g["-f"] = (at(1, 1), at(3, 1), n, "-")
            r = {
                "+2": (at(3, 0), n, "+"),
                "-2": (at(3, 1), n, "-"),
                "+x": (at(1, 1), n, "+"),
                "+s": (at(1, 0), n, "+"),
                "-x": (at(2, 0), n, "-"),
                "-s": (at(2, 1), n, "-"),
                "p": (at(0, 1), n, "p"),
            }
        else:
            g["+f"] = (at(2, 0), at(3, 0), h, "+")
            g["-f"] = (at(1, 0) + h, at(3, 0) + h, h, "-")
            g["p-"] = (at(2, 0), at(2, 1), n, "p")
            g["p+"] = (at(1, 0), at(1, 1), n, "p")
            g["pl"] = (at(3, 0), at(3, 1), h, "p")
            g["pu"] = (at(3, 0) + h, at(3, 1) + h, h, "p")
            r = {
                "p2": (at(3, 1), n, "p"),
                "p+": (at(1, 1), n, "p"),
                "p-": (at(2, 1), n, "p"),
                "p": (at(0, 1), n, "p"),
                "+2": (at(3, 0), h, "+"),
                "-2": (at(3, 0) + h, h, "-"),
                "+s": (at(1, 0), n, "+"),
                "-s": (at(2, 0), n, "-"),
            }
        for name, entry in g.items():
            gather[t, name] = (len(gather), e, *entry)
        for name, entry in r.items():
            reduce[t, name] = (len(reduce), e, *entry)
    rows = {}
    total = 0
    for key, (_, _, _, n, _) in reduce.items():
        rows[key] = total
        total += n
    return gather, reduce, rows, total


GATHER, REDUCE, LANDING, LANDING_ROWS = plan()


def iota(shape, dim):
    return lax.broadcasted_iota(jnp.int32, shape, dim)


def dot(a, b):
    return jnp.dot(a, b, preferred_element_type=F32)


def remote(src, dst, send, recv, device):
    return pltpu.make_async_remote_copy(
        src_ref=src,
        dst_ref=dst,
        send_sem=send,
        recv_sem=recv,
        device_id=device,
        device_id_type=MESH,
    )


def kernel(
    tok, gain, q, k, v, ids, rw, gp, up, dp,
    att_out, mix_out,
    normed, there, back, stack, sb, ab, xg, pb, wg, wu, wd, rb, fb, cb, rows_in, share,
    qb, kb, vb, smk, smv, ob, ao,
    w_sem, d_send, d_recv, c_send, c_recv, g_send, g_recv, r_send, r_recv,
    a_send, a_recv, s_send, s_recv, o_send, o_recv,
):
    me_s = lax.axis_index("seq")
    me_p = lax.axis_index("exp")
    me_y = lax.div(me_s, 2)
    me_z = lax.rem(me_s, 2)
    core = lax.rem(me_p, 2)
    chip = lax.div(me_p, 2)
    half = lax.div(me_p, 16)
    slot = lax.rem(me_p, 16)
    seg = 2 * me_s + core
    peer = {
        "+": (2 * lax.rem(me_y + 1, 4) + me_z, me_p),
        "-": (2 * lax.rem(me_y + 3, 4) + me_z, me_p),
        "p": (2 * me_y + 1 - me_z, me_p),
    }

    barrier = pltpu.get_barrier_semaphore()

    def greet_exp(j, carry):
        to = lax.rem(me_z * 32 + me_p + j, 64)
        pl.semaphore_signal(
            barrier, inc=1, device_id=(2 * me_y + lax.div(to, 32), lax.rem(to, 32)),
            device_id_type=MESH,
        )
        return carry

    def greet_seq(j, carry):
        other = lax.rem(2 * me_y + j, 8)
        pl.semaphore_signal(barrier, inc=1, device_id=(other, me_p), device_id_type=MESH)
        pl.semaphore_signal(
            barrier, inc=1, device_id=(other, me_p + 1 - 2 * core), device_id_type=MESH
        )
        return carry

    lax.fori_loop(1, 64, greet_exp, 0)
    lax.fori_loop(2, 8, greet_seq, 0)

    weights = [
        pltpu.make_async_copy(src, dst.at[:, pl.ds(0, FFD), :], w_sem.at[i])
        for i, (src, dst) in enumerate(((gp, wg), (up, wu), (dp, wd)))
    ]
    for copy in weights:
        copy.start()

    row_j = iota((128, 64), 0)
    expert_j = 2 * (row_j % 32) + row_j // 64
    first = ids[0:1, :] == expert_j
    second = ids[1:2, :] == expert_j
    named = (first | second).astype(F32)
    above = (iota((64, 64), 0) < iota((64, 64), 1)).astype(BF)
    before = dot(named.astype(BF), above)
    pick = jnp.where(before == ((row_j // 32) % 2).astype(F32), named, 0.0)

    def norm_rows(i, carry):
        rows = pl.ds(pl.multiple_of(i * 16, 16), 16)
        vals = tok[rows, :].astype(F32)
        inv = lax.rsqrt(jnp.mean(vals * vals, axis=-1, keepdims=True) + EPS)
        normed[rows, :] = (vals * inv * gain[...]).astype(BF)
        return carry

    lax.fori_loop(0, 4, norm_rows, 0)

    out_i, in_i = iota((512, 512), 0), iota((512, 512), 1)
    there[...] = (in_i == (out_i % 16) * 32 + out_i // 16).astype(BF)
    back[...] = (in_i == (out_i % 32) * 16 + out_i // 32).astype(BF)

    for c in range(8):
        cols = slice(c * 512, c * 512 + 512)
        picked = dot(pick.astype(BF), normed[:, cols]).astype(BF)
        for t in range(4):
            for d in range(2):
                place = slice((2 * c + d) * 32, (2 * c + d) * 32 + 32)
                stack[t, place, :] = picked[32 * t : 32 * t + 32, d * W : d * W + W]
    for t in range(4):
        sb[t] = dot(there[...], stack[t]).astype(BF)

    pl.semaphore_wait(barrier, 75)

    def block_of(index):
        return pl.ds(pl.multiple_of(index * 16, 16), 16)

    me_x = lax.div(me_p, 8)
    me_h = lax.rem(lax.div(me_p, 2), 4)
    own_place = 2 * me_x + core

    def owner_of(j):
        to = lax.rem(me_p + j, 32)
        delta = lax.rem(lax.rem(lax.div(to, 2), 4) + 4 - me_h, 4)
        low = jnp.where(delta == 1, 0, jnp.where(delta == 3, 1, 1 - me_z))
        low = jnp.where(delta == 0, me_z, low)
        group = jnp.where(delta == 2, 3, jnp.where(low == me_z, 1, 2))
        group = jnp.where(delta == 0, 0, group)
        return to, 2 * me_y + low, 8 * group + own_place

    def source_of(j):
        place = lax.rem(own_place + j, 32)
        group = lax.div(place, 8)
        delta = jnp.where(group == 0, 0, jnp.where(group == 3, 2, 1 + 2 * me_z))
        low = jnp.where(group < 2, me_z, 1 - me_z)
        high = lax.rem(me_h + 4 - delta, 4)
        column = lax.div(lax.rem(place, 8), 2) * 8 + high * 2 + lax.rem(place, 2)
        return place, 2 * me_y + low, column

    def go_out(t, start):
        def step(j, carry):
            to, row, place = owner_of(j)
            copy = remote(
                sb.at[t, block_of(to), :], ab.at[t, block_of(place), :],
                d_send.at[t, to], d_recv.at[t, place], (row, to),
            )
            if start:
                copy.start()
            else:
                copy.wait_send()
            return carry

        lax.fori_loop(1, 32, step, 0)

    def go_home(t, start):
        def step(j, carry):
            place, row, column = source_of(j)
            copy = remote(
                fb.at[t, block_of(place), :], cb.at[t, block_of(me_p), :],
                c_send.at[t, place], c_recv.at[t, me_p], (row, column),
            )
            if start:
                copy.start()
            else:
                copy.wait_send()
            return carry

        lax.fori_loop(1, 32, step, 0)

    def came(t, dst, recv, own):
        def step(j, carry):
            place = lax.rem(own + j, 32)
            ref = dst.at[t, block_of(place), :]
            remote(ref, ref, d_send.at[t, place], recv.at[t, place], peer["p"]).wait_recv()
            return carry

        lax.fori_loop(1, 32, step, 0)

    go_out(0, True)
    go_out(1, True)

    part = jnp.where(first, rw[0:1, :], 0.0) + jnp.where(second, rw[1:2, :], 0.0)
    part = part * pick
    big = part.astype(BF)
    small = (part - big.astype(F32)).astype(BF)
    eye = (iota((64, 64), 0) == iota((64, 64), 1)).astype(BF)
    share[0] = lax.dot_general(eye, big, NT, preferred_element_type=F32).astype(BF)
    share[1] = lax.dot_general(eye, small, NT, preferred_element_type=F32).astype(BF)
    for t in range(4):
        ab[t, block_of(own_place), :] = sb[t, block_of(me_p), :]

    def zero_rows(i, carry):
        rows = pl.ds(pl.multiple_of(FFD + i * 16, 16), 16)
        for e in range(2):
            for ref in (wg, wu, wd):
                ref[e, rows, :] = jnp.zeros((16, D), BF)
        return carry

    lax.fori_loop(0, 5, zero_rows, 0)

    def cols_of(index):
        return pl.ds(pl.multiple_of(index * 128, 128), 128)

    def toks_of(index):
        return pl.ds(pl.multiple_of(index * 64, 64), 64)

    def heads_start(j, carry):
        m = lax.rem(chip + j, 16)
        to = 2 * m + half
        for i, (src, dst) in enumerate(((k, kb), (v, vb), (q, qb))):
            piece, land = src.at[:, cols_of(m)], dst.at[toks_of(slot), :]

            @pl.when(to != me_p)
            def _():
                remote(piece, land, a_send.at[i, m], a_recv.at[i, slot], (me_s, to)).start()

            @pl.when(to == me_p)
            def _():
                pltpu.make_async_copy(piece, land, a_recv.at[i, slot]).start()

        return carry

    def heads_wait(j, carry):
        for i, dst in enumerate((kb, vb, qb)):
            land = dst.at[toks_of(j), :]
            pltpu.make_async_copy(land, land, a_recv.at[i, j]).wait()
        return carry

    def heads_sent(j, carry):
        for i, (src, dst) in enumerate(((k, kb), (v, vb), (q, qb))):

            @pl.when(2 * j + half != me_p)
            def _():
                remote(
                    src.at[:, cols_of(j)], dst.at[toks_of(slot), :],
                    a_send.at[i, j], a_recv.at[i, slot], (me_s, 2 * j + half),
                ).wait_send()

        return carry

    def sort_rows(t):
        came(t, ab, d_recv, own_place)
        e, off, n, _ = STREAMS[t]
        rows = dot(back[...], ab[t]).astype(BF)
        for c in range(16):
            xg[e, off : off + n, c * W : c * W + W] = rows[32 * c : 32 * c + 32]

    def gather(t, name):
        i, e, src, dst, n, way = GATHER[t, name]
        return remote(
            xg.at[e, pl.ds(src, n), :], xg.at[e, pl.ds(dst, n), :],
            g_send.at[i], g_recv.at[i], peer[way],
        )

    def spread(t, *names):
        for name in names:
            gather(t, name).start()

    def arrived(t, *names):
        for name in names:
            i, e, _, dst, n, way = GATHER[t, name]
            ref = xg.at[e, pl.ds(dst, n), :]
            remote(ref, ref, g_send.at[i], g_recv.at[i], peer[way]).wait_recv()

    def summarize():
        blocks = (iota((64, 1024), 1) // 16 == iota((64, 1024), 0)).astype(BF)
        mine = toks_of(seg)
        smk[mine, :] = (dot(blocks, kb[...]) * 0.25).astype(BF)
        smv[mine, :] = (dot(blocks, vb[...]) * 0.25).astype(BF)

    def sums(g, src_seg):
        other = (lax.div(g, 2), 2 * chip + lax.rem(g, 2))
        for i, ref in enumerate((smk, smv)):
            yield remote(
                ref.at[toks_of(src_seg), :], ref.at[toks_of(src_seg), :],
                s_send.at[i, g], s_recv.at[i, src_seg], other,
            )

    def sums_start(g, carry):
        for copy in sums(g, seg):
            copy.start()
        return carry

    def sums_sent(g, carry):
        for copy in sums(g, seg):
            copy.wait_send()
        return carry

    def sums_wait(g, carry):
        for copy in sums(g, g):
            copy.wait_recv()
        return carry

    def sums_zero(g, carry):
        smk[toks_of(g), :] = jnp.zeros((64, 128), BF)
        smv[toks_of(g), :] = jnp.zeros((64, 128), BF)
        return carry

    def attend(step, carry):
        rows = pl.ds(pl.multiple_of(lax.div(step, 2) * 128, 128), 128)
        head = lax.rem(step, 2)
        lane = iota((128, 128), 1) // 64 == head
        query = jnp.where(lane, qb[rows, :].astype(F32) * 0.125, 0.0).astype(BF)
        local = lax.dot_general(query, kb[...], NT, preferred_element_type=F32)
        summ = lax.dot_general(query, smk[...], NT, preferred_element_type=F32)
        pos = lax.div(step, 2) * 128 + iota((128, 1024), 0)
        col = iota((128, 1024), 1)
        local = jnp.where(col <= pos, local, NEG)
        summ = jnp.where(col < seg * 64, summ, NEG)
        top = jnp.maximum(
            jnp.max(local, axis=-1, keepdims=True), jnp.max(summ, axis=-1, keepdims=True)
        )
        local = jnp.exp(local - top)
        summ = jnp.exp(summ - top)
        total = jnp.sum(local, axis=-1, keepdims=True) + jnp.sum(summ, axis=-1, keepdims=True)
        mixed = (dot(local.astype(BF), vb[...]) + dot(summ.astype(BF), smv[...])) / total
        ob[rows, :] = jnp.where(lane, mixed, ob[rows, :].astype(F32)).astype(BF)
        return carry

    def back_start(j, carry):
        i = lax.rem(slot + j, 16)
        to = 16 * core + i
        piece, land = ob.at[toks_of(i), :], ao.at[:, cols_of(chip)]

        @pl.when(to != me_p)
        def _():
            remote(piece, land, o_send.at[i], o_recv.at[chip], (me_s, to)).start()

        @pl.when(to == me_p)
        def _():
            pltpu.make_async_copy(piece, land, o_recv.at[chip]).start()

        return carry

    def back_wait(m, carry):
        land = ao.at[:, cols_of(m)]
        pltpu.make_async_copy(land, land, o_recv.at[m]).wait()
        return carry

    def back_sent(i, carry):
        @pl.when(16 * core + i != me_p)
        def _():
            remote(
                ob.at[toks_of(i), :], ao.at[:, cols_of(chip)],
                o_send.at[i], o_recv.at[chip], (me_s, 16 * core + i),
            ).wait_send()

        return carry

    def expert(e, group):
        rows = pl.ds(pl.multiple_of(group * 128, 128), 128)
        gate = jnp.zeros((128, FFP), F32)
        high = jnp.zeros((128, FFP), F32)
        for c in range(4):
            cols = slice(c * 1024, c * 1024 + 1024)
            part = xg[e, rows, cols]
            gate += lax.dot_general(part, wg[e, :, cols], NT, preferred_element_type=F32)
            high += lax.dot_general(part, wu[e, :, cols], NT, preferred_element_type=F32)
        hidden = (gate / (1.0 + jnp.exp(-gate)) * high).astype(BF)
        for c in range(8):
            cols = slice(c * 512, c * 512 + 512)
            pb[e, rows, cols] = dot(hidden, wd[e, :, cols]).astype(BF)

    def experts(e, first, groups):
        def step(i, carry):
            expert(e, first + i)
            return carry

        lax.fori_loop(0, groups, step, 0)

    def landing(t, name):
        i, e, src, n, way = REDUCE[t, name]
        return rb.at[pl.ds(LANDING[t, name], n), :]

    def reduce(t, name):
        i, e, src, n, way = REDUCE[t, name]
        return remote(
            pb.at[e, pl.ds(src, n), :], landing(t, name), r_send.at[i], r_recv.at[i], peer[way]
        )

    def send(t, *names):
        for name in names:
            reduce(t, name).start()

    def landed(t, *names):
        for name in names:
            i, _, _, _, way = REDUCE[t, name]
            ref = landing(t, name)
            remote(ref, ref, r_send.at[i], r_recv.at[i], peer[way]).wait_recv()

    def add_into(t, name, *terms, skip=0):
        _, e, first, _, _ = REDUCE[t, name]
        n = REDUCE[t, terms[0]][3]

        def step(i, carry):
            rows = pl.ds(pl.multiple_of(first + skip + i * 16, 16), 16)
            total = pb[e, rows, :].astype(F32)
            for term in terms:
                start = pl.multiple_of(LANDING[t, term] + i * 16, 16)
                total += rb[pl.ds(start, 16), :].astype(F32)
            pb[e, rows, :] = total.astype(BF)
            return carry

        lax.fori_loop(0, n // 16, step, 0)

    def finish(t, *terms):
        e, off, n, _ = STREAMS[t]
        landed(t, *terms)

        def step(i, carry):
            rows = pl.ds(pl.multiple_of(off + i * 16, 16), 16)
            total = pb[e, rows, :].astype(F32)
            for term in terms:
                start = pl.multiple_of(LANDING[t, term] + i * 16, 16)
                total += rb[pl.ds(start, 16), :].astype(F32)
            total = total.astype(BF)
            for c in range(16):
                place = pl.ds(pl.multiple_of(c * 32 + i * 16, 16), 16)
                stack[t, place, :] = total[:, c * W : c * W + W]
            return carry

        lax.fori_loop(0, n // 16, step, 0)
        fb[t] = dot(there[...], stack[t]).astype(BF)
        go_home(t, True)
        cb[t, block_of(me_p), :] = fb[t, block_of(own_place), :]

    def collect(t):
        came(t, cb, c_recv, me_p)
        rows = dot(back[...], cb[t]).astype(BF)
        for c in range(16):
            rows_in[32 * t : 32 * t + 32, c * W : c * W + W] = rows[32 * c : 32 * c + 32]

    sort_rows(0)
    spread(0, "p", "+o", "-o")
    go_out(2, True)
    sort_rows(1)
    spread(1, "p", "+o", "-o")
    go_out(3, True)
    arrived(0, "+o")
    spread(0, "+f")
    arrived(0, "p")
    spread(0, "+x", "-x")
    arrived(1, "+o")
    spread(1, "+f")
    sort_rows(2)
    spread(2, "p", "+o", "-o")
    arrived(1, "p")
    spread(1, "+x", "-x")
    for copy in weights:
        copy.wait()
    experts(0, 0, 1)
    sort_rows(3)
    spread(3, "+o", "-o", "p")
    lax.fori_loop(0, 16, heads_start, 0)
    arrived(0, "-o", "-x")
    spread(0, "-f")
    arrived(2, "+o")
    spread(2, "+f")
    arrived(2, "p")
    spread(2, "+x", "-x")
    arrived(1, "-o", "-x")
    spread(1, "-f")
    arrived(3, "+o")
    spread(3, "+f", "p-")
    arrived(3, "-o")
    spread(3, "-f", "p+")
    arrived(3, "p")
    experts(1, 0, 1)
    arrived(0, "+x")
    arrived(1, "+x")
    experts(0, 1, 2)
    arrived(2, "-o", "-x")
    spread(2, "-f")
    arrived(3, "+f")
    spread(3, "pl")
    arrived(3, "-f")
    spread(3, "pu")
    arrived(0, "+f", "-f")
    arrived(1, "+f", "-f")
    experts(0, 3, 1)
    send(0, "+2", "-2", "+x", "-x")
    arrived(2, "+x")
    arrived(3, "p-", "p+")
    experts(1, 1, 2)
    lax.fori_loop(0, 16, heads_wait, 0)
    summarize()
    lax.fori_loop(seg + 1, 16, sums_start, 0)
    lax.fori_loop(seg + 1, 16, sums_zero, 0)
    ob[...] = jnp.zeros((1024, 128), BF)
    arrived(2, "+f", "-f")
    arrived(3, "pl", "pu")
    experts(1, 3, 1)
    send(3, "p2", "p+", "p-")
    send(1, "+2", "-2", "+x", "-x")
    send(3, "p")
    landed(0, "+2")
    add_into(0, "+s", "+2")
    send(0, "+s")
    landed(0, "-2")
    add_into(0, "-s", "-2")
    send(0, "-s")
    send(2, "+2", "-2", "+x", "-x")
    for t in range(4):
        go_out(t, False)
    lax.fori_loop(0, 16, heads_sent, 0)
    lax.fori_loop(0, seg, sums_wait, 0)
    lax.fori_loop(0, 12, attend, 0)
    landed(1, "+2")
    add_into(1, "+s", "+2")
    send(1, "+s")
    landed(1, "-2")
    add_into(1, "-s", "-2")
    send(1, "-s")
    landed(0, "+x", "-s")
    add_into(0, "p", "+x", "-s")
    send(0, "p")
    lax.fori_loop(12, 16, attend, 0)
    lax.fori_loop(0, 16, back_start, 0)
    landed(3, "p2")
    add_into(3, "+2", "p2")
    send(3, "+2", "-2")
    landed(2, "+2")
    add_into(2, "+s", "+2")
    send(2, "+s")
    landed(2, "-2")
    add_into(2, "-s", "-2")
    send(2, "-s")
    landed(3, "p+", "p-")
    add_into(3, "+s", "p+")
    add_into(3, "-s", "p-")
    landed(1, "+x", "-s")
    add_into(1, "p", "+x", "-s")
    send(1, "p")
    landed(3, "+2")
    add_into(3, "+s", "+2")
    send(3, "+s")
    landed(3, "-2")
    add_into(3, "-s", "-2", skip=16)
    send(3, "-s")
    finish(0, "+s", "-x", "p")
    landed(2, "+x", "-s")
    add_into(2, "p", "+x", "-s")
    send(2, "p")
    finish(1, "+s", "-x", "p")
    finish(2, "+s", "-x", "p")
    collect(0)
    finish(3, "p", "+s", "-s")
    lax.fori_loop(0, 16, back_wait, 0)
    att_out[...] = ao[...]
    collect(1)
    collect(2)
    for t in range(3):
        go_home(t, False)
    collect(3)
    for c in range(8):
        cols = slice(c * 512, c * 512 + 512)
        mix = dot(share[0], rows_in[:, cols]) + dot(share[1], rows_in[:, cols])
        mix_out[:, cols] = mix.astype(BF)
    go_home(3, False)
    lax.fori_loop(0, 16, back_sent, 0)
    lax.fori_loop(seg + 1, 16, sums_sent, 0)
    for t, name in GATHER:
        gather(t, name).wait_send()
    for t, name in REDUCE:
        reduce(t, name).wait_send()


def on_device(tokens, gain, queries, keys, values, ids, rw, gate, up, down):
    vmem = pl.BlockSpec(memory_space=pltpu.VMEM)
    hbm = pl.BlockSpec(memory_space=pl.ANY)
    dma = pltpu.SemaphoreType.DMA
    head = pltpu.VMEM((1024, 128), BF)
    block = pltpu.VMEM((4, 512, W), BF)
    return pl.pallas_call(
        kernel,
        out_shape=(
            jax.ShapeDtypeStruct((64, 2048), BF),
            jax.ShapeDtypeStruct((64, D), BF),
        ),
        in_specs=[vmem, vmem, hbm, hbm, hbm, vmem, vmem, hbm, hbm, hbm],
        out_specs=(vmem, vmem),
        scratch_shapes=[
            pltpu.VMEM((64, D), BF),
            pltpu.VMEM((512, 512), BF),
            pltpu.VMEM((512, 512), BF),
            block,
            block,
            block,
            pltpu.VMEM((2, 512, D), BF),
            pltpu.VMEM((2, 512, D), BF),
            pltpu.VMEM((2, FFP, D), BF),
            pltpu.VMEM((2, FFP, D), BF),
            pltpu.VMEM((2, FFP, D), BF),
            pltpu.VMEM((LANDING_ROWS, D), BF),
            block,
            block,
            pltpu.VMEM((128, D), BF),
            pltpu.VMEM((2, 64, 128), BF),
            head,
            head,
            head,
            head,
            head,
            head,
            pltpu.VMEM((64, 2048), BF),
            dma((3,)),
            dma((4, 32)),
            dma((4, 32)),
            dma((4, 32)),
            dma((4, 32)),
            dma((len(GATHER),)),
            dma((len(GATHER),)),
            dma((len(REDUCE),)),
            dma((len(REDUCE),)),
            dma((3, 16)),
            dma((3, 16)),
            dma((2, 16)),
            dma((2, 16)),
            dma((16,)),
            dma((16,)),
        ],
        compiler_params=pltpu.CompilerParams(
            collective_id=0, has_side_effects=True, vmem_limit_bytes=60 * 1024 * 1024
        ),
        name="layer",
    )(tokens, gain.reshape(1, D), queries, keys, values, ids.T, rw.T, gate, up, down)


def solution(mesh):
    rows = P(("seq", "exp"), None)
    parts = P("exp", "seq", None)
    return jax.shard_map(
        on_device,
        mesh=mesh,
        in_specs=(rows, P(), rows, rows, rows, rows, rows, parts, parts, parts),
        out_specs=(rows, rows),
        check_vma=False,
    )
```
